256 devices in a mesh: zone: 16 (over x, y), tile: 16 (over z, core).
Axes of the slice: x: 4, y: 4, z: 8, core: 2. Of those that a mesh axis runs over, the one named last changes fastest.
Arguments:
- strips: bfloat16 [12288, 8, 13, 256], P(('zone', 'tile')), may hold values from -6 to 6
- footprint: int32 [12288, 1], P(('zone', 'tile')), may hold values from 0 to 15; in each aligned block of 48 rows (0 to 47, 48 to 95, ...) at most 7 rows name the same one
- row_block: int32 [12288], P(('zone', 'tile')), may hold values from 0 to 7
- date_slot: int32 [12288], P(('zone', 'tile')), may hold values from 0 to 11
- quality: int32 [12288], P(('zone', 'tile')), may hold values from 0 to 3
- date_gain: float32 [12], replicated, may hold values from 0.3 to 3
- reprojection: bfloat16 [256, 128], replicated, may hold values from -0.2 to 0.7
- stem_weight: bfloat16 [13, 128], replicated, may hold values from -1.75 to 1.75
- stem_bias: float32 [128], replicated, may hold values from -3 to 3
- depth_near: bfloat16 [9, 128], replicated, may hold values from -2 to 2
- gain_near: float32 [128], replicated, may hold values from 0.5 to 1.5
- up_near: bfloat16 [128, 512], replicated, may hold values from -0.5 to 0.5
- down_near: bfloat16 [512, 128], replicated, may hold values from -0.25 to 0.25
- depth_far: bfloat16 [9, 128], replicated, may hold values from -2 to 2
- gain_far: float32 [128], replicated, may hold values from 0.5 to 1.5
- up_far: bfloat16 [128, 512], replicated, may hold values from -0.5 to 0.5
- down_far: bfloat16 [512, 128], replicated, may hold values from -0.25 to 0.25
- class_weight: bfloat16 [128, 11], replicated, may hold values from -8 to 8
- class_bias: float32 [11], replicated, may hold values from -4 to 4
Outputs:
- probs: float32 [1024, 11, 2048], P('zone', None, 'tile')
The draws below stay inside these ranges and needn't reach their ends.
Inputs may be any that keep to these rules, and one draw needn't show every extreme that they name: `footprint`: in the rows of one device no tile is named by more than 7 strips.
All inputs are finite; a program needn't handle non-finite values.
Results may differ from the reference program's by a relative error of at most 0.015.
Values may be sent and summed in bfloat16 or wider, within the bound.
A program may use at most 64 MiB of HBM per device.

```python
import math
import jax
import jax.numpy as jnp
import numpy as np
from jax import lax

BANDS = 13
PIX = 256
LINES = 8
CH = 128
HID = 512
CLASSES = 11
DATES = 12
S_DEV = 48
TROWS = 64
OPIX = 128
RB = 8
CAP = 7
STRIPS = 12288
N_ZONE = 16
N_TILE = 16


def draw_reprojection(key, part):
    rows = jnp.arange(PIX, dtype=jnp.int32)[:, None]
    cols = jnp.arange(OPIX, dtype=jnp.int32)[None, :]
    band = jnp.where(rows * OPIX // PIX == cols, 0.5, 0.0).astype(jnp.float32)
    spread = 0.6 / math.sqrt(PIX)
    noise = jax.random.normal(key, (PIX, OPIX), jnp.float32) * spread
    noise = jnp.clip(noise, -0.19, 0.19)
    return (band + noise).astype(jnp.bfloat16)


def draw_class_weight(key, part):
    first_key = jax.random.fold_in(key, 11)
    scale = 2.0 / math.sqrt(CH)
    table = jax.random.normal(first_key, (CH, CLASSES), jnp.float32) * scale
    return jnp.clip(table, -8.0, 8.0).astype(jnp.bfloat16)


def touch_ends(drawn, stream_key, smallest, top_value):
    index_at = [jax.random.randint(jax.random.fold_in(stream_key, axis), (), 0, length) for axis, length in enumerate(drawn.shape)]
    longest = drawn.shape.index(max(drawn.shape))
    next_to = index_at[:longest] + [(index_at[longest] + 1) % drawn.shape[longest]] + index_at[longest + 1:]
    return drawn.at[tuple(index_at)].set(smallest).at[tuple(next_to)].set(top_value)


def steps_of(rng, shape, split, smallest, top_value):
    loudness = 1.0
    for dim, shards_of in split:
        heights = jax.random.uniform(jax.random.fold_in(jax.random.fold_in(rng, 6), dim), (shards_of,), jnp.float32, smallest / len(split), top_value / len(split))
        loudness = loudness * jnp.repeat(jnp.exp(heights), shape[dim] // shards_of).reshape((-1,) + (1,) * (len(shape) - 1 - dim))
    return loudness


def deal_out(key, own, number, rows, count, top, most, slope):
    ranking = jax.random.permutation(key, count)
    crowded, ordinary = load_shares(count, rows * top, most, slope, True), load_shares(count, rows * top, most, slope, False)
    places = jnp.arange(count)

    def named(lengths, turn):
        used = int((lengths > 0).sum())
        fixed = max(1, used // 4)
        moved = fixed + (places - fixed + turn * (used - fixed)) % max(1, count - fixed)
        return jnp.zeros((count,), jnp.int32).at[ranking[jnp.where(places < fixed, places, moved)]].set(jnp.asarray(lengths, jnp.int32))

    lengths = jnp.where(number % 4 == 0, named(crowded, number // 4), named(ordinary, number - number // 4 - 1))
    mixed = jax.random.permutation(jax.random.fold_in(own, 3), count)
    giver, sink = mixed[0:count // 2 * 2:2], mixed[1:count // 2 * 2:2]
    margin = jnp.minimum(lengths[giver] - 1, most - lengths[sink]) // 2
    margin = jnp.where((giver == ranking[0]) | (sink == ranking[0]) | (lengths[sink] == 0), 0, jnp.maximum(margin, 0))
    moved = jax.random.randint(jax.random.fold_in(own, 4), (count // 2,), 0, 1 << 20) % (margin + 1)
    lengths = lengths.at[giver].add(-moved).at[sink].add(moved)
    members = jnp.searchsorted(jnp.cumsum(lengths), jnp.arange(rows * top), side="right").astype(jnp.int32)
    table = members.reshape(top, rows).T
    table = table[jax.random.permutation(jax.random.fold_in(own, 1), rows)]
    turn = jax.random.randint(jax.random.fold_in(own, 2), (rows, 1), 0, top)
    return jnp.take_along_axis(table, (jnp.arange(top)[None, :] + turn) % top, axis=1)


def load_shares(number_of, total, most, skew, full):
    loads = [(1 << 20) // math.isqrt(grade ** skew) + 1 for grade in range(1, number_of + 1)]
    largest = most if full else min(most, max(-(-total // number_of), total * loads[0] // sum(loads)))
    least = 1 if total - largest >= number_of - 1 else 0
    given, spare = [largest] + [least] * (number_of - 1), total - largest - least * (number_of - 1)
    while spare > 0:
        free = [i for i in range(1, number_of) if given[i] < largest] or [i for i in range(1, number_of) if given[i] < most]
        mass, budget = sum([loads[i] for i in free]), spare
        for i in free:
            more = min(most - given[i], max(1, budget * loads[i] // mass), spare)
            given[i] = given[i] + more
            spare = spare - more
    return np.array(given)


def gaussian(own_key, shape, deviation, bound, shards=(), held_as=jnp.bfloat16):
    array = deviation * jax.random.normal(own_key, shape, jnp.float32)
    if shards:
        array = array * steps_of(own_key, shape, shards, -0.22, 0.18)
    return jnp.clip(array, -bound, bound).astype(held_as)


def setup_inputs(seed: int = 0) -> dict:
    splits = jax.random.split(jax.random.key(seed), 20)
    strips = gaussian(splits[0], (STRIPS, LINES, BANDS, PIX), 1.0, 6.0, ((0, 256),))
    footprint_keys = jax.random.split(jax.random.fold_in(splits[1], 1), STRIPS // S_DEV)
    footprint_turns = jax.random.permutation(jax.random.fold_in(splits[1], 3), STRIPS // S_DEV)
    footprint = jax.vmap(lambda own, number: deal_out(jax.random.fold_in(splits[1], 2), own, number, S_DEV, N_TILE, 1, CAP, 2))(footprint_keys, footprint_turns).reshape((STRIPS, 1))
    row_block = touch_ends(jax.random.randint(splits[2], (STRIPS,), 0, RB), jax.random.fold_in(splits[2], 1), 0, RB - 1).astype(jnp.int32)
    date_slot = touch_ends(jax.random.randint(splits[3], (STRIPS,), 0, DATES), jax.random.fold_in(splits[3], 1), 0, DATES - 1).astype(jnp.int32)
    quality = touch_ends(jax.random.randint(splits[4], (STRIPS,), 0, 4), jax.random.fold_in(splits[4], 1), 0, 3).astype(jnp.int32)
    date_gain = jnp.clip(jnp.exp(jax.random.uniform(splits[5], (DATES,), jnp.float32, math.log(0.3), math.log(3.0))), 0.3, 3.0)
    reprojection = draw_reprojection(jax.random.fold_in(splits[19], 71), 0)
    stem_weight = gaussian(splits[7], (BANDS, CH), BANDS ** -0.5, 1.75)
    stem_bias = gaussian(splits[8], (CH,), 0.5, 3.0, (), jnp.float32)
    depth_near = gaussian(splits[9], (9, CH), 9 ** -0.5, 2.0)
    gain_near = jnp.clip(1.0 + 0.1 * jax.random.normal(splits[10], (CH,), jnp.float32), 0.5, 1.5)
    up_near = gaussian(splits[11], (CH, HID), CH ** -0.5, 0.5)
    down_near = gaussian(splits[12], (HID, CH), HID ** -0.5, 0.25)
    depth_far = gaussian(splits[13], (9, CH), 9 ** -0.5, 2.0)
    gain_far = jnp.clip(1.0 + 0.1 * jax.random.normal(splits[14], (CH,), jnp.float32), 0.5, 1.5)
    up_far = gaussian(splits[15], (CH, HID), CH ** -0.5, 0.5)
    down_far = gaussian(splits[16], (HID, CH), HID ** -0.5, 0.25)
    class_weight = draw_class_weight(jax.random.fold_in(splits[19], 71), 0)
    class_bias = gaussian(splits[18], (CLASSES,), 1.0, 4.0, (), jnp.float32)
    return {"strips": strips, "footprint": footprint, "row_block": row_block, "date_slot": date_slot, "quality": quality, "date_gain": date_gain, "reprojection": reprojection, "stem_weight": stem_weight, "stem_bias": stem_bias, "depth_near": depth_near, "gain_near": gain_near, "up_near": up_near, "down_near": down_near, "depth_far": depth_far, "gain_far": gain_far, "up_far": up_far, "down_far": down_far, "class_weight": class_weight, "class_bias": class_bias}


def convnext(features, padded, depth, gain, up, down, reach):
    rows = features.shape[0]
    chans = features.shape[1]
    cols = features.shape[2]

    def one_block(index):
        start = (index * 8).astype(jnp.int32)
        window = lax.dynamic_slice_in_dim(padded, start, 8 + 2 * reach, 0).astype(jnp.float32)
        current = lax.dynamic_slice_in_dim(features, start, 8, 0).astype(jnp.float32)
        total = jnp.zeros((8, chans, cols), jnp.float32)
        for shift_row in range(3):
            for shift_col in range(3):
                tap = depth[shift_row * 3 + shift_col].astype(jnp.float32)[None, :, None]
                total = total + tap * window[shift_row * reach:shift_row * reach + 8, :, shift_col * reach:shift_col * reach + cols]
        average = lax.optimization_barrier(jnp.mean(total, axis=1, keepdims=True))
        centred = total - average
        spread = lax.optimization_barrier(jnp.mean(centred * centred, axis=1, keepdims=True))
        normed = (centred * lax.rsqrt(spread + 1e-05) * gain.astype(jnp.float32)[None, :, None]).astype(jnp.bfloat16)
        hidden = jax.nn.gelu(jnp.einsum('rco,ch->rho', normed.astype(jnp.float32), up.astype(jnp.float32)), approximate=True).astype(jnp.bfloat16)
        return (current + jnp.einsum('rho,hc->rco', hidden.astype(jnp.float32), down.astype(jnp.float32))).astype(jnp.bfloat16)
    pieces = lax.map(one_block, jnp.arange(rows // 8, dtype=jnp.int32))
    return pieces.reshape(rows, chans, cols)

def reference(strips, footprint, row_block, date_slot, quality, date_gain, reprojection, stem_weight, stem_bias, depth_near, gain_near, up_near, down_near, depth_far, gain_far, up_far, down_far, class_weight, class_bias):
    date_hit = date_slot[:, None] == jnp.arange(DATES, dtype=jnp.int32)[None, :]
    gain_each = lax.optimization_barrier(jnp.sum(jnp.where(date_hit, date_gain.astype(jnp.float32)[None, :], 0.0), axis=1))
    strip_weight = (quality.astype(jnp.float32) / 3.0 * gain_each).astype(jnp.bfloat16)
    group_size = N_TILE * S_DEV

    def zone_composite(group):
        start = (group * group_size).astype(jnp.int32)
        chosen = lax.dynamic_slice_in_dim(strips, start, group_size, 0).reshape(group_size * LINES * BANDS, PIX)
        projected = jnp.dot(chosen, reprojection, preferred_element_type=jnp.float32).astype(jnp.bfloat16)
        projected = projected.reshape(group_size, LINES * BANDS, OPIX)
        weights = lax.dynamic_slice_in_dim(strip_weight, start, group_size, 0).astype(jnp.float32)
        owners = lax.dynamic_slice_in_dim(footprint[:, 0], start, group_size, 0)
        blocks = lax.dynamic_slice_in_dim(row_block, start, group_size, 0)
        segment = (owners * RB + blocks).astype(jnp.int32)
        numerator = jax.ops.segment_sum(weights[:, None, None] * projected.astype(jnp.float32), segment, num_segments=N_TILE * RB)
        denominator = jax.ops.segment_sum(weights, segment, num_segments=N_TILE * RB)
        composite = (numerator / jnp.maximum(denominator, 1.0)[:, None, None]).astype(jnp.bfloat16)
        return composite.reshape(N_TILE, TROWS, BANDS, OPIX)
    tiles = lax.map(zone_composite, jnp.arange(N_ZONE, dtype=jnp.int32))
    image = tiles.transpose(0, 2, 3, 1, 4).reshape(N_ZONE * TROWS, BANDS, N_TILE * OPIX)
    features0 = (jnp.einsum('rbo,bc->rco', image.astype(jnp.float32), stem_weight.astype(jnp.float32)) + stem_bias.astype(jnp.float32)[None, :, None]).astype(jnp.bfloat16)
    padded0 = jnp.pad(features0, ((1, 1), (0, 0), (1, 1)))
    features1 = convnext(features0, padded0, depth_near, gain_near, up_near, down_near, 1)
    padded1 = jnp.pad(features1, ((2, 2), (0, 0), (2, 2)))
    features2 = convnext(features1, padded1, depth_far, gain_far, up_far, down_far, 2)
    logits = jnp.einsum('rco,ck->rko', features2.astype(jnp.float32), class_weight.astype(jnp.float32)) + class_bias.astype(jnp.float32)[None, :, None]
    return jax.nn.softmax(logits, axis=1)
```

```python
import jax
import jax.numpy as jnp
from jax import lax
from jax.experimental import pallas as pl
from jax.experimental.pallas import tpu as pltpu
from jax.sharding import PartitionSpec as P

F32 = jnp.float32
BF16 = jnp.bfloat16
MESH = pl.DeviceIdType.MESH

N_ZONE = 16
N_TILE = 16
NZ = 8
S = 48
LINES = 8
BANDS = 13
ROWS = 64
RB = 8
CELL = LINES * BANDS
DEN = 16
TILE = DEN + RB * CELL
STEP = 8
CHUNKS = ((0, 224), (224, 208), (432, 208), (640, 208))
HALO = 3
EXT = ROWS + 2 * HALO
MID = ROWS + 4
GROUP1 = 4
GROUP2 = 4


def bin_kernel(fp, rb, ds, q, dg, strips, reproj, out, acc, den):
    step = pl.program_id(0)

    @pl.when(step == 0)
    def _():
        def clear(c, carry):
            acc[c] = jnp.zeros((BANDS, LINES, 128), F32)
            den[c] = jnp.zeros((8, 128), F32)
            return carry

        lax.fori_loop(0, N_TILE * RB, clear, 0)

    p = jnp.dot(strips[...], reproj[...], preferred_element_type=F32)
    for i in range(STEP):
        s = step * STEP + i
        cell = fp[s] * RB + rb[s]
        gain = dg[ds[s]]
        quality = jnp.full((8, 128), q[s], jnp.int32).astype(F32)
        w = (quality / 3.0 * jnp.full((8, 128), gain, F32)).astype(BF16).astype(F32)
        part = p[i * CELL : (i + 1) * CELL, :].reshape(BANDS, LINES, 128)
        acc[cell] = acc[cell] + w[None] * part
        den[cell] = den[cell] + w

    @pl.when(step == S // STEP - 1)
    def _():
        def put(t, carry):
            rows = [den[t * RB + r][0:1, :] for r in range(RB)]
            d = jnp.concatenate(rows, axis=0)
            hi = d.astype(BF16).astype(F32)
            out[t, 0:DEN, :] = jnp.concatenate([hi, d - hi], axis=0).astype(BF16)
            out[t, DEN:TILE, :] = (
                acc[pl.ds(t * RB, RB)].reshape(RB * CELL, 128).astype(BF16)
            )
            return carry

        lax.fori_loop(0, N_TILE, put, 0)


def binned(strips, footprint, row_block, date_slot, quality, date_gain, reprojection):
    smem = pl.BlockSpec(memory_space=pltpu.SMEM)
    return pl.pallas_call(
        bin_kernel,
        grid=(S // STEP,),
        in_specs=[
            smem,
            smem,
            smem,
            smem,
            smem,
            pl.BlockSpec((STEP * CELL, 256), lambda i: (i, 0)),
            pl.BlockSpec((256, 128), lambda i: (0, 0)),
        ],
        out_specs=pl.BlockSpec((N_TILE, TILE, 128), lambda i: (0, 0, 0)),
        out_shape=jax.ShapeDtypeStruct((N_TILE, TILE, 128), BF16),
        scratch_shapes=[
            pltpu.VMEM((N_TILE * RB, BANDS, LINES, 128), F32),
            pltpu.VMEM((N_TILE * RB, 8, 128), F32),
        ],
        name="bin_strips",
    )(footprint, row_block, date_slot, quality, date_gain, strips, reprojection)


def ring_plan(d):
    first, second = ((0, 1), (2, 3)) if d == 0 else ((2, 3), (0, 1))
    order = [(4, c) for c in first]
    for k in (3, 2, 1):
        order += [(k, c) for c in second + first]
    return first, order


def added(parts, chunk):
    total = parts[0].astype(F32)
    for part in parts[1:]:
        total = total + part.astype(F32)
    return total


def ring_kernel(
    x, comp, eto, etr, pair, sb, rv, rowf, ef, es, rh, er, psend, precv, rsend, rrecv, hsend, hrecv
):
    zone = lax.axis_index("zone")
    tile = lax.axis_index("tile")
    z = tile // 2
    core = tile - 2 * z
    other = 1 - core

    def at(dz, dt):
        return (lax.rem(zone + dz + N_ZONE, N_ZONE), lax.rem(tile + dt + N_TILE, N_TILE))

    barrier = pltpu.get_barrier_semaphore()
    friends = [(0, 1), (0, -1), (0, 2), (0, -2), (1, -1), (1, 0), (1, 1), (-1, -1), (-1, 0), (-1, 1)]
    for dz, dt in friends:
        pl.semaphore_signal(barrier, inc=1, device_id=at(dz, dt), device_id_type=MESH)
    pl.semaphore_wait(barrier, len(friends))

    partner = (zone, 2 * z + other)

    def owner(o):
        return lax.rem(z + o, NZ)

    pair_order = (4, 3, 5, 2, 6, 1, 7, 0)
    pair_copies = {}
    for o in pair_order:
        copy = pltpu.make_async_remote_copy(
            src_ref=x.at[2 * owner(o) + other],
            dst_ref=pair.at[o],
            send_sem=psend.at[o],
            recv_sem=precv.at[o],
            device_id=partner,
            device_id_type=MESH,
        )
        copy.start()
        pair_copies[o] = copy

    rowf[...] = jnp.ones_like(rowf)
    ef[...] = jnp.ones_like(ef)

    plans = [ring_plan(0), ring_plan(1)]
    have = set()
    copies = {}

    def need_pair(o):
        if o not in have:
            pair_copies[o].wait_recv()
            have.add(o)

    def gathered(o, c, arrived):
        r0, n = CHUNKS[c]
        parts = [x[2 * owner(o) + core, r0 : r0 + n, :], pair[o, r0 : r0 + n, :]]
        return added(parts + arrived, c)

    for i in range(14):
        for d in (0, 1):
            first, order = plans[d]
            k, c = order[i]
            r0, n = CHUNKS[c]
            o = k if d == 0 else (NZ - k) % NZ
            need_pair(o)
            arrived = []
            if k < 3 or (k == 3 and c in first):
                copies[d, k + 1, c].wait_recv()
                arrived = [rv[d, k, r0 : r0 + n, :]]
            total = gathered(o, c, arrived)
            if c == 0:
                both = total[0:8] + total[8:16]
                high = both.astype(BF16).astype(F32)
                sb[d, k - 1, 0:DEN, :] = jnp.concatenate([high, both - high], axis=0).astype(BF16)
                sb[d, k - 1, DEN : r0 + n, :] = total[DEN:].astype(BF16)
            else:
                sb[d, k - 1, r0 : r0 + n, :] = total.astype(BF16)
            copy = pltpu.make_async_remote_copy(
                src_ref=sb.at[d, k - 1, pl.ds(r0, n)],
                dst_ref=rv.at[d, k - 1, pl.ds(r0, n)],
                send_sem=rsend.at[d, k - 1, c],
                recv_sem=rrecv.at[d, k - 1, c],
                device_id=at(0, 2 if d == 0 else -2),
                device_id_type=MESH,
            )
            copy.start()
            copies[d, k, c] = copy

    need_pair(0)
    inverse = None
    for c in (0, 2, 1, 3):
        r0, n = CHUNKS[c]
        for d in (0, 1):
            copies[d, 1, c].wait_recv()
        total = gathered(0, c, [rv[0, 0, r0 : r0 + n, :], rv[1, 0, r0 : r0 + n, :]])
        if c == 0:
            inverse = 1.0 / jnp.maximum(total[0:8] + total[8:16], 1.0)
            total = total[DEN:]
        for h in (0, 1):
            rb = 2 * c + h
            value = total[h * CELL : (h + 1) * CELL] * inverse[rb : rb + 1]
            first_row = 16 * (LINES * rb + HALO)
            for b in range(BANDS):
                rowf[pl.ds(first_row + b, LINES, stride=16), :] = value[LINES * b : LINES * (b + 1)]
        a = 16 * c + HALO
        comp[a : a + 16] = rowf[16 * a : 16 * (a + 16), :].astype(BF16).reshape(16, 16, 128)

    which = lax.broadcasted_iota(jnp.int32, (16, 128), 0)
    lane = lax.broadcasted_iota(jnp.int32, (16, 128), 1)
    select = jnp.where(lane == jnp.where(which < 4, which, which + 120), 1.0, 0.0)
    select = jnp.where(which < 8, select, 0.0).astype(BF16)
    for b in range(BANDS):
        plane = rowf[pl.ds(b, 128, stride=16), :].astype(BF16)
        edge = lax.dot_general(select, plane, (((1,), (1,)), ((), ())), preferred_element_type=F32)
        ef[pl.ds(b, 8, stride=16), :] = edge[0:8]
    es[...] = ef[...].astype(BF16).reshape(8, 16, 128)

    sends = []

    def send(src, dst, where):
        n = len(sends)
        copy = pltpu.make_async_remote_copy(
            src_ref=src,
            dst_ref=dst,
            send_sem=hsend.at[n],
            recv_sem=hrecv.at[n],
            device_id=where,
            device_id_type=MESH,
        )
        copy.start()
        sends.append(copy)

    send(comp.at[pl.ds(HALO + ROWS - 3, 3)], rh.at[0], at(1, 0))
    send(comp.at[pl.ds(HALO, 3)], rh.at[1], at(-1, 0))
    for dz in (1, -1, 0):
        send(es.at[pl.ds(5, 3)], er.at[1 - dz], at(dz, 1))
        send(es.at[pl.ds(0, 3)], er.at[3 + 1 - dz], at(dz, -1))
    eto[...] = es[...]
    for copy in sends:
        copy.wait_recv()
    comp[0:HALO] = rh[0]
    comp[HALO + ROWS : EXT] = rh[1]
    etr[...] = er[...].reshape(18, 16, 128)
    for copy in list(pair_copies.values()) + list(copies.values()) + sends:
        copy.wait_send()


def composited(x):
    vmem = pl.BlockSpec(memory_space=pltpu.VMEM)
    dma = pltpu.SemaphoreType.DMA
    return pl.pallas_call(
        ring_kernel,
        in_specs=[vmem],
        out_specs=[vmem] * 3,
        out_shape=[
            jax.ShapeDtypeStruct((EXT, 16, 128), BF16),
            jax.ShapeDtypeStruct((8, 16, 128), BF16),
            jax.ShapeDtypeStruct((18, 16, 128), BF16),
        ],
        scratch_shapes=[
            pltpu.VMEM((NZ, TILE, 128), BF16),
            pltpu.VMEM((2, 4, TILE, 128), BF16),
            pltpu.VMEM((2, 4, TILE, 128), BF16),
            pltpu.VMEM((16 * 136, 128), F32),
            pltpu.VMEM((128, 128), F32),
            pltpu.VMEM((8, 16, 128), BF16),
            pltpu.VMEM((2, 3, 16, 128), BF16),
            pltpu.VMEM((6, 3, 16, 128), BF16),
            dma((NZ,)),
            dma((NZ,)),
            dma((2, 4, 4)),
            dma((2, 4, 4)),
            dma((8,)),
            dma((8,)),
        ],
        compiler_params=pltpu.CompilerParams(collective_id=0, has_side_effects=True),
        name="ring_composite",
    )(x)


def gelu2(v):
    inner = v * (0.7978845608028654 + 0.035677408136300125 * (v * v))
    return v + v * jnp.tanh(inner)


def pointwise(dw, x, gain, up, down):
    mean = jnp.mean(dw, axis=0, keepdims=True)
    centred = dw - mean
    var = jnp.mean(centred * centred, axis=0, keepdims=True)
    normed = (centred * lax.rsqrt(var + 1e-5) * gain).astype(BF16)
    hidden = gelu2(jnp.dot(up[...], normed, preferred_element_type=F32).astype(BF16))
    return x + jnp.dot(down[...], hidden, preferred_element_type=F32)


def column(row):
    return jnp.broadcast_to(row, (128, 128)).T


def block_kernel(
    comp, eto, etr, stem, bias, k1, g1, u1, d1, k2, g2, u2, d2, cw, cb,
    out,
    wf, w1, w1t, up1, dn1, up2, dn2, gain1, gain2, taps, cls, three, ethree, edges, hpack, feats,
):
    zone = lax.axis_index("zone")
    tile = lax.axis_index("tile")
    top, bottom = zone == 0, zone == N_ZONE - 1
    left, right = tile == 0, tile == N_TILE - 1

    bias_row = bias[...].reshape(1, 128)
    stem_f = stem[...].astype(F32)

    def stem_rows(k, tap, lanes):
        k0 = k * 16
        wf[k0 : k0 + BANDS, lanes] = stem_f * tap if tap is not None else stem_f
        b = bias_row * tap if tap is not None else bias_row
        for j in range(3):
            part = b.astype(BF16).astype(F32)
            wf[k0 + BANDS + j : k0 + BANDS + j + 1, lanes] = part
            b = b - part

    for target, swap in ((w1, False), (w1t, True)):
        wf[...] = jnp.zeros_like(wf)
        for i in range(3):
            for j in range(3):
                tap = k1[3 * i + j : 3 * i + j + 1, :].astype(F32)
                stem_rows(3 * j + i if swap else 3 * i + j, tap, slice(0, 128))
        stem_rows(4, None, slice(128, 256))
        target[...] = wf[...].T.astype(BF16)
    up1[...] = u1[...].astype(F32).T.astype(BF16)
    up2[...] = u2[...].astype(F32).T.astype(BF16)
    dn1[...] = (0.5 * d1[...].astype(F32)).T.astype(BF16)
    dn2[...] = (0.5 * d2[...].astype(F32)).T.astype(BF16)
    gain1[...] = column(g1[...].reshape(1, 128))
    gain2[...] = column(g2[...].reshape(1, 128))
    diagonal = lax.broadcasted_iota(jnp.int32, (128, 128), 0) == lax.broadcasted_iota(jnp.int32, (128, 128), 1)
    for t in range(9):
        tap = jnp.broadcast_to(k2[t : t + 1, :].astype(F32), (128, 128))
        taps[:, t * 128 : (t + 1) * 128] = jnp.where(diagonal, tap, 0.0).astype(BF16)
    wf[0:16, 0:128] = jnp.zeros((16, 128), F32)
    wf[0:11, 0:128] = cw[...].astype(F32)
    cls[...] = wf[0:16, 0:128].astype(BF16)

    def row_of(q):
        v = comp[q].astype(F32)
        if q < HALO:
            v = jnp.where(top, 0.0, v)
        if q >= HALO + ROWS:
            v = jnp.where(bottom, 0.0, v)
        return v

    lane16 = lax.broadcasted_iota(jnp.int32, (16, 128), 1)
    lane = lax.broadcasted_iota(jnp.int32, (128, 128), 1)
    low = jnp.where(top, HALO, 0)
    high = jnp.where(bottom, HALO + ROWS, EXT)
    inside16 = (lane16 >= low) & (lane16 < high)
    inside = (lane >= low) & (lane < high)

    def edge_column(side, j):
        parts = [etr[(3 * side + s) * 3 + j].astype(F32) for s in range(3)]
        before = pltpu.roll(parts[0], 64, axis=1)
        after = pltpu.roll(parts[2], 64, axis=1)
        whole = jnp.where(lane16 < HALO, before, jnp.where(lane16 < HALO + ROWS, parts[1], after))
        gone = left if side == 0 else right
        return jnp.where(inside16 & jnp.logical_not(gone), whole, 0.0)

    def own_column(k):
        v = eto[k].astype(F32)
        o = 0 if k == 0 else 127
        for q in (0, 1, 2, EXT - 3, EXT - 2, EXT - 1):
            shifted = pltpu.roll(row_of(q), (q - o) % 128, axis=1)
            v = jnp.where(lane16 == q, shifted, v)
        return jnp.where(inside16, v, 0.0)

    lefts = [edge_column(0, j) for j in range(3)] + [own_column(0)]
    rights = [own_column(7)] + [edge_column(1, j) for j in range(3)]
    for n, v in enumerate(lefts + rights):
        ethree[n, 0:16] = pltpu.roll(v, 1, axis=1).astype(BF16)
        ethree[n, 16:32] = v.astype(BF16)
        ethree[n, 32:48] = pltpu.roll(v, 127, axis=1).astype(BF16)
    before, after = lefts[2], rights[1]
    for q in range(EXT):
        v = row_of(q)
        lv = jnp.where(lane16 == 0, pltpu.roll(before, (-q) % 128, axis=1), pltpu.roll(v, 1, axis=1))
        rv = jnp.where(lane16 == 127, pltpu.roll(after, (127 - q) % 128, axis=1), pltpu.roll(v, 127, axis=1))
        three[q, 0:16] = lv.astype(BF16)
        three[q, 16:32] = v.astype(BF16)
        three[q, 32:48] = rv.astype(BF16)

    def first(parts, w):
        xs = jnp.concatenate(parts, axis=1)
        n = len(parts)
        y = jnp.dot(w[:, 0:144], xs, preferred_element_type=F32)
        gain = jnp.concatenate([gain1[...]] * n, axis=1)
        x0 = y[128:256].astype(BF16).astype(F32)
        return pointwise(y[0:128], x0, gain, up1, dn1)

    parts = [ethree[n : n + 3].reshape(144, 128) for n in (0, 1, 4, 5)]
    y = first(parts, w1t)
    for n, gone in enumerate((left, left, right, right)):
        keep = inside & jnp.logical_not(gone)
        edges[n * 128 : (n + 1) * 128] = jnp.where(keep, y[:, n * 128 : (n + 1) * 128], 0.0).astype(BF16)
    row = lax.broadcasted_iota(jnp.int32, (128, 384), 0)
    slot = lax.broadcasted_iota(jnp.int32, (128, 384), 1)
    packed = jnp.zeros((128, 384), F32)
    for n, place in enumerate((2, 3, 0, 1)):
        pick = jnp.where(slot == 4 * (row - 1) + place, 1.0, 0.0).astype(BF16)
        packed = packed + jnp.dot(edges[n * 128 : (n + 1) * 128], pick, preferred_element_type=F32)
    for g in range(3):
        hpack[g] = packed[:, g * 128 : (g + 1) * 128]

    def block1(it, carry):
        q0 = it * GROUP1
        y = first([three[pl.ds(q0 + n, 3)].reshape(144, 128) for n in range(GROUP1)], w1)
        for n in range(GROUP1):
            q = q0 + n
            v = y[:, n * 128 : (n + 1) * 128]
            out_of_grid = (top & (q < 2)) | (bottom & (q >= 2 + ROWS))
            v = jnp.where(out_of_grid, 0.0, v)
            side = pltpu.roll(hpack[q // 32], 126 - 4 * lax.rem(q, 32), axis=1)
            feats[q, 0] = jnp.where(lane < 2, side, pltpu.roll(v, 2, axis=1)).astype(BF16)
            feats[q, 1] = v.astype(BF16)
            feats[q, 2] = jnp.where(lane >= 126, side, pltpu.roll(v, 126, axis=1)).astype(BF16)
        return carry

    lax.fori_loop(0, MID // GROUP1, block1, 0)

    k16 = lax.broadcasted_iota(jnp.int32, (16, 128 * GROUP2), 0)
    cbias = jnp.full((16, 128 * GROUP2), -1e30, F32)
    for k in range(11):
        cbias = jnp.where(k16 == k, cb[k], cbias)

    def block2(it, carry):
        q0 = it * GROUP2
        around = []
        for i in range(3):
            for j in range(3):
                around.append(jnp.concatenate([feats[q0 + n + 2 * i, j] for n in range(GROUP2)], axis=1))
        dw = jnp.dot(taps[...], jnp.concatenate(around, axis=0), preferred_element_type=F32)
        x = jnp.concatenate([feats[q0 + 2 + n, 1] for n in range(GROUP2)], axis=1).astype(F32)
        gain = jnp.concatenate([gain2[...]] * GROUP2, axis=1)
        y = pointwise(dw, x, gain, up2, dn2).astype(BF16)
        logits = jnp.dot(cls[...], y, preferred_element_type=F32) + cbias
        e = jnp.exp(logits - jnp.max(logits, axis=0, keepdims=True))
        probs = e / jnp.sum(e, axis=0, keepdims=True)
        for n in range(GROUP2):
            out[pl.ds(q0 + n, 11, stride=ROWS), :] = probs[0:11, n * 128 : (n + 1) * 128]
        return carry

    lax.fori_loop(0, ROWS // GROUP2, block2, 0)


def classified(comp, eto, etr, *weights):
    vmem = pl.BlockSpec(memory_space=pltpu.VMEM)
    return pl.pallas_call(
        block_kernel,
        in_specs=[vmem] * 14 + [pl.BlockSpec(memory_space=pltpu.SMEM)],
        out_specs=vmem,
        out_shape=jax.ShapeDtypeStruct((11 * ROWS, 128), F32),
        scratch_shapes=[
            pltpu.VMEM((256, 256), F32),
            pltpu.VMEM((256, 256), BF16),
            pltpu.VMEM((256, 256), BF16),
            pltpu.VMEM((512, 128), BF16),
            pltpu.VMEM((128, 512), BF16),
            pltpu.VMEM((512, 128), BF16),
            pltpu.VMEM((128, 512), BF16),
            pltpu.VMEM((128, 128), F32),
            pltpu.VMEM((128, 128), F32),
            pltpu.VMEM((128, 9 * 128), BF16),
            pltpu.VMEM((16, 128), BF16),
            pltpu.VMEM((EXT, 48, 128), BF16),
            pltpu.VMEM((8, 48, 128), BF16),
            pltpu.VMEM((512, 128), BF16),
            pltpu.VMEM((3, 128, 128), F32),
            pltpu.VMEM((MID, 3, 128, 128), BF16),
        ],
        name="blocks",
    )(comp, eto, etr, *weights)


def shards(
    strips,
    footprint,
    row_block,
    date_slot,
    quality,
    date_gain,
    reprojection,
    stem_weight,
    stem_bias,
    depth_near,
    gain_near,
    up_near,
    down_near,
    depth_far,
    gain_far,
    up_far,
    down_far,
    class_weight,
    class_bias,
):
    rows = jnp.transpose(strips, (0, 2, 1, 3)).reshape(S * CELL, 256)
    x = binned(rows, footprint.reshape(S), row_block, date_slot, quality, date_gain, reprojection)
    comp, eto, etr = composited(x)
    probs = classified(
        comp,
        eto,
        etr,
        stem_weight,
        stem_bias,
        depth_near,
        gain_near,
        up_near,
        down_near,
        depth_far,
        gain_far,
        up_far,
        down_far,
        class_weight.T,
        class_bias,
    )
    return jnp.transpose(probs.reshape(11, ROWS, 128), (1, 0, 2))


def solution(mesh):
    each = P(("zone", "tile"))
    in_specs = (
        P(("zone", "tile"), None, None, None),
        P(("zone", "tile"), None),
        each,
        each,
        each,
    ) + (P(),) * 14
    return jax.shard_map(
        shards, mesh=mesh, in_specs=in_specs, out_specs=P("zone", None, "tile"), check_vma=False
    )
```
